32 devices in a mesh: groups: 2 (over x), level: 16 (over z, y, core).
Axes of the slice: x: 2, y: 2, z: 4, core: 2. Of those that a mesh axis runs over, the one named last changes fastest.
Arguments:
- latents: bfloat16 [64, 256, 640], P(('groups', 'level')), parts along dimension 0, may hold values from -6 to 6
- levels: int32 [64], P(('groups', 'level')), parts along dimension 0, may hold values from 0 to 15
- back_reach: int32 [64], P(('groups', 'level')), parts along dimension 0, may hold values from 1 to 2
- text_ids: int32 [154], P('groups'), parts along dimension 0, may hold values from 0 to 49407
- text_table: bfloat16 [49408, 1024], P('level'), may hold values from -6 to 6
- text_proj: bfloat16 [1024, 640], replicated, may hold values from -0.75 to 0.75
- level_embed: float32 [16, 640], replicated, may hold values from -3 to 3
- step_rate: float32 [16], replicated, may hold values from 0.3 to 1
- norm_gain: float32 [640], replicated, may hold values from 0.5 to 1.5
- w_query: bfloat16 [640, 640], replicated
- w_key: bfloat16 [640, 640], replicated
- w_value: bfloat16 [640, 640], replicated, may hold values from -0.25 to 0.25
- w_out: bfloat16 [640, 640], replicated, may hold values from -0.25 to 0.25
Outputs:
- queue_out: bfloat16 [64, 256, 640], P(('groups', 'level')), parts along dimension 0
The draws below stay inside these ranges and needn't reach their ends.
There are 2 independent parts, one for each index of `groups`. The reference program is written for one: setup_inputs(seed, part) draws one part's arguments, and reference() takes and returns one part's arrays. A program takes and returns all parts, laid end to end along the dimension named above; an argument that names none is the same for every part. Nothing has to cross between parts.
All inputs are finite; a program needn't handle non-finite values.
Results may differ from the reference program's by a relative error of at most 0.007.
Values may be sent and summed in bfloat16 or wider, within the bound.
A program may use at most 64 MiB of HBM per device.

```python
import math
import jax
import jax.numpy as jnp
import numpy as np
from jax import lax

C = 640
DH = 64
P_SIZE = 256
F_DEV = 2
BAND = 2
LEVELS = 16
STEPS = 3
VOCAB = 49408
CTXW = 1024
NTEXT = 77
FRAMES = 32


def query_key_pair(key):
    base = jax.random.normal(jax.random.fold_in(key, 7), (C, C), jnp.float32) / math.sqrt(C)
    other = jax.random.normal(jax.random.fold_in(key, 11), (C, C), jnp.float32) / math.sqrt(C)
    first = base
    second = other
    return (first, second)


def draw_w_query(key, part):
    return query_key_pair(key)[0].astype(jnp.bfloat16)


def draw_w_key(key, part):
    return query_key_pair(key)[1].astype(jnp.bfloat16)


def touch_ends(result, stream_key, low, high):
    shape = result.shape
    spot = [jax.random.randint(jax.random.fold_in(stream_key, axis), (), 0, shape[axis]) for axis in range(len(shape))]
    result = result.at[tuple(spot)].set(low)
    longest = shape.index(max(shape))
    spot[longest] = (spot[longest] + 1) % shape[longest]
    return result.at[tuple(spot)].set(high)


def steps_of(stream_key, dims, pieces, smallest, largest):
    loudness, own = 1.0, jax.random.fold_in(stream_key, 6)
    for dim, parts in pieces:
        draws = jnp.exp(jax.random.uniform(jax.random.fold_in(own, dim), (parts,), jnp.float32, smallest / len(pieces), largest / len(pieces)))
        loudness = loudness * jnp.repeat(draws, dims[dim] // parts).reshape([-1 if axis == dim else 1 for axis in range(len(dims))])
    return loudness


def rank_table(amount, slope):
    loads = [(1 << 20) // math.isqrt(standing ** slope) + 1 for standing in range(1, amount + 1)]
    width = 1 + sum(loads) // (1 << 30)
    return np.cumsum(np.array([max(1, weight // width) for weight in loads]))


def ranked(rng, shape, number_of, lean):
    grid = rank_table(number_of, lean)
    lot = jax.random.randint(jax.random.fold_in(rng, 1), shape, 0, int(grid[number_of - 1]))
    standing = jnp.searchsorted(jnp.asarray(grid, jnp.int32), lot, side="right")
    return jax.random.permutation(jax.random.fold_in(rng, 2), number_of)[standing].astype(jnp.int32)


def noise(stream_key, extent, width, most, shards=(), kind=jnp.bfloat16):
    result = width * jax.random.normal(stream_key, extent, jnp.float32)
    if shards:
        result = result * steps_of(stream_key, extent, shards, -0.22, 0.18)
    return jnp.clip(result, -most, most).astype(kind)


def setup_inputs(seed: int = 0, part: int = 0) -> dict:
    arg_keys = jax.random.split(jax.random.key(seed), 14)
    own_keys = jax.random.split(jax.random.fold_in(arg_keys[13], part), 14)
    latents = noise(own_keys[0], (FRAMES, P_SIZE, C), 1.0, 6.0, ((0, 16),))
    levels = touch_ends(jax.random.randint(own_keys[1], (FRAMES,), 0, LEVELS), jax.random.fold_in(own_keys[1], 1), 0, LEVELS - 1).astype(jnp.int32)
    back_reach = touch_ends(jax.random.randint(own_keys[2], (FRAMES,), 1, BAND + 1), jax.random.fold_in(own_keys[2], 1), 1, BAND).astype(jnp.int32)
    text_ids = touch_ends(ranked(own_keys[3], (NTEXT,), VOCAB, 2), jax.random.fold_in(own_keys[3], 3), 0, VOCAB - 1).astype(jnp.int32)
    text_table = noise(arg_keys[4], (VOCAB, CTXW), 1.0, 6.0, ((0, 16),))
    text_proj = noise(arg_keys[5], (CTXW, C), (CTXW // 16) ** -0.5, 0.75)
    level_embed = noise(arg_keys[6], (LEVELS, C), 0.5, 3.0, (), jnp.float32)
    step_rate = jnp.clip(jnp.exp(jax.random.uniform(arg_keys[7], (LEVELS,), jnp.float32, math.log(0.3), math.log(1.0))), 0.3, 1.0)
    norm_gain = jnp.clip(1.0 + 0.1 * jax.random.normal(arg_keys[8], (C,), jnp.float32), 0.5, 1.5)
    w_query = draw_w_query(jax.random.fold_in(arg_keys[13], 71), part)
    w_key = draw_w_key(jax.random.fold_in(arg_keys[13], 71), part)
    w_value = noise(arg_keys[11], (C, C), C ** -0.5, 0.25)
    w_out = noise(arg_keys[12], (C, C), C ** -0.5, 0.25)
    return {"latents": latents, "levels": levels, "back_reach": back_reach, "text_ids": text_ids, "text_table": text_table, "text_proj": text_proj, "level_embed": level_embed, "step_rate": step_rate, "norm_gain": norm_gain, "w_query": w_query, "w_key": w_key, "w_value": w_value, "w_out": w_out}


def reference(latents, levels, back_reach, text_ids, text_table, text_proj, level_embed, step_rate, norm_gain, w_query, w_key, w_value, w_out):
    pooled = lax.optimization_barrier(jnp.mean(text_table[text_ids].astype(jnp.float32), axis=0))
    text_vec = jnp.dot(pooled.astype(jnp.bfloat16)[None, :], text_proj, preferred_element_type=jnp.float32)[0]
    cond = level_embed[levels] + text_vec[None, :]
    rate = step_rate[levels]
    frames = latents.shape[0]
    heads = C // DH
    frame_index = jnp.arange(frames, dtype=jnp.int32)
    scale = 1.0 / DH ** 0.5
    current = latents
    for step in range(STEPS):
        hin = current.astype(jnp.float32) + cond[:, None, :]
        normed = (hin * lax.rsqrt(lax.optimization_barrier(jnp.mean(hin * hin, axis=-1, keepdims=True)) + 1e-06) * norm_gain).astype(jnp.bfloat16)
        flat = normed.reshape(-1, C)
        query = jnp.dot(flat, w_query, preferred_element_type=jnp.float32).astype(jnp.bfloat16).reshape(frames, P_SIZE, heads, DH)
        keys = jnp.dot(flat, w_key, preferred_element_type=jnp.float32).astype(jnp.bfloat16).reshape(frames, P_SIZE, heads, DH)
        values = jnp.dot(flat, w_value, preferred_element_type=jnp.float32).astype(jnp.bfloat16).reshape(frames, P_SIZE, heads, DH)
        pad_keys = jnp.pad(keys, ((BAND, BAND), (0, 0), (0, 0), (0, 0)))
        pad_values = jnp.pad(values, ((BAND, BAND), (0, 0), (0, 0), (0, 0)))
        query_f = query.astype(jnp.float32)
        score_list = []
        valid_list = []
        for offset in range(-BAND, BAND + 1):
            shifted = pad_keys[BAND + offset:BAND + offset + frames].astype(jnp.float32)
            raw = jnp.einsum('fphd,fphd->fph', query_f, shifted) * scale
            valid = (offset >= -back_reach) & (frame_index + offset >= 0) & (frame_index + offset < frames)
            score_list.append(jnp.where(valid[:, None, None], raw, -1e+30))
            valid_list.append(valid.astype(jnp.float32)[:, None, None])
        scores = jnp.stack(score_list)
        masks = jnp.stack(valid_list)
        top = lax.optimization_barrier(jnp.max(scores, axis=0))
        expo = jnp.exp(scores - top[None]) * masks
        weights = (expo / lax.optimization_barrier(jnp.sum(expo, axis=0))[None]).astype(jnp.bfloat16)
        attended = jnp.zeros((frames, P_SIZE, heads, DH), jnp.float32)
        for slot, offset in enumerate(range(-BAND, BAND + 1)):
            shifted = pad_values[BAND + offset:BAND + offset + frames].astype(jnp.float32)
            attended = attended + weights[slot].astype(jnp.float32)[..., None] * shifted
        attended = attended.astype(jnp.bfloat16).reshape(-1, C)
        noise_pred = jnp.dot(attended, w_out, preferred_element_type=jnp.float32).reshape(frames, P_SIZE, C)
        updated = (current.astype(jnp.float32) - rate[:, None, None] * noise_pred).astype(jnp.bfloat16)
        current = jnp.roll(updated, F_DEV, axis=0)
    return current
```

```python
import functools

import jax
import jax.numpy as jnp
from jax import lax
from jax.experimental import pallas as pl
from jax.experimental.pallas import tpu as pltpu
from jax.sharding import PartitionSpec as P

DH = 64
BAND = 2
STEPS = 3
SPAN = 2 * BAND + 1
MESH = pl.DeviceIdType.MESH


def queue_kernel(
    n,
    x_hbm,
    level_hbm,
    reach_hbm,
    ids_hbm,
    table_hbm,
    proj_hbm,
    embed_hbm,
    srate_hbm,
    gain_hbm,
    wq_hbm,
    wk_hbm,
    wv_hbm,
    wo_hbm,
    out_hbm,
    recv,
    xa,
    xb,
    xo,
    q_s,
    k_s,
    v_s,
    part,
    att,
    table,
    proj,
    embed,
    gain_s,
    wq,
    wk,
    wv,
    wo,
    wqp,
    wkp,
    wvp,
    wop,
    level_s,
    reach_s,
    ids_s,
    srate_s,
    pool,
    metas,
    cond,
    rate,
    mask,
    perm,
    unperm,
    gather,
    x_send,
    x_recv,
    p_send,
    p_recv,
    m_send,
    m_recv,
    o_send,
    o_recv,
    local,
):
    me = lax.axis_index("level")
    fdev = x_hbm.shape[0]
    halves, frames, pos, width = recv.shape
    rows = frames * pos
    pad = BAND * pos
    barrier = pltpu.get_barrier_semaphore()
    for hop in range(1, n):
        pl.semaphore_signal(
            barrier, inc=1, device_id={"level": lax.rem(me + hop, n)}, device_id_type=MESH
        )
    mine = pl.ds(me * fdev, fdev)
    pairs = [
        (level_hbm, level_s),
        (reach_hbm, reach_s),
        (ids_hbm, ids_s),
        (srate_hbm, srate_s),
        (table_hbm, table),
        (embed_hbm, embed),
        (gain_hbm, gain_s),
        (proj_hbm, proj),
        (wq_hbm, wq),
        (wk_hbm, wk),
        (wv_hbm, wv),
        (wo_hbm, wo),
    ] + [(x_hbm.at[:, me, h], recv.at[h, mine]) for h in range(halves)]
    stage = [
        pltpu.make_async_copy(src, dst, local.at[slot]) for slot, (src, dst) in enumerate(pairs)
    ]
    for copy in stage:
        copy.start()

    def x_copy(h, peer, owner):
        return pltpu.make_async_remote_copy(
            src_ref=x_hbm.at[:, peer, h],
            dst_ref=recv.at[h, pl.ds(owner * fdev, fdev)],
            send_sem=x_send.at[h, peer],
            recv_sem=x_recv.at[h, owner],
            device_id={"level": peer},
            device_id_type=MESH,
        )

    def p_copy(peer, owner):
        return pltpu.make_async_remote_copy(
            src_ref=pool.at[owner],
            dst_ref=pool.at[owner],
            send_sem=p_send.at[peer],
            recv_sem=p_recv.at[owner],
            device_id={"level": peer},
            device_id_type=MESH,
        )

    def m_copy(peer, owner):
        return pltpu.make_async_remote_copy(
            src_ref=metas.at[owner],
            dst_ref=metas.at[owner],
            send_sem=m_send.at[peer],
            recv_sem=m_recv.at[owner],
            device_id={"level": peer},
            device_id_type=MESH,
        )

    def o_copy(h, section, owner, peer):
        return pltpu.make_async_remote_copy(
            src_ref=xo.at[h, pl.ds(section * fdev, fdev)],
            dst_ref=out_hbm.at[:, owner, h],
            send_sem=o_send.at[h, peer],
            recv_sem=o_recv.at[h, owner],
            device_id={"level": peer},
            device_id_type=MESH,
        )

    def flip(bits):
        other = me
        for place in range(n.bit_length()):
            if bits >> place & 1:
                bit = lax.rem(lax.div(me, 1 << place), 2)
                other = other + (1 - 2 * bit) * (1 << place)
        return other

    peers = [flip(bits) for bits in range(1, n)]
    pl.semaphore_wait(barrier, n - 1)
    early = n // 2
    for peer in peers[:early]:
        x_copy(0, peer, me).start()

    stage[0].wait()
    stage[1].wait()
    lane = lax.broadcasted_iota(jnp.int32, (1, 128), 1)
    fact = jnp.zeros((1, 128), jnp.int32)
    for f in range(fdev):
        fact = jnp.where(lane == f, level_s[f], fact)
        fact = jnp.where(lane == fdev + f, reach_s[f], fact)
    metas[me] = fact
    for peer in peers:
        m_copy(peer, me).start()

    vocab = table.shape[0]
    stage[2].wait()
    first_id = me * vocab
    spots = lax.broadcasted_iota(jnp.int32, (1, vocab), 1) + first_id
    counts = jnp.zeros((1, vocab), jnp.float32)
    text_tokens = ids_s.shape[0]
    for token in range(text_tokens):
        counts = counts + jnp.where(spots == ids_s[token], 1.0, 0.0)
    counts = jnp.broadcast_to(counts, (16, vocab)).astype(jnp.bfloat16)
    stage[4].wait()
    partial = jnp.dot(counts, table[...], preferred_element_type=jnp.float32)
    pool[me] = partial[0:1]
    for peer in peers:
        p_copy(peer, me).start()
    for peer in peers[early:]:
        x_copy(0, peer, me).start()
    for h in range(1, halves):
        for peer in peers:
            x_copy(h, peer, me).start()

    heads = width // DH
    per = 128 // heads
    wide = k_s.shape[1]
    blocks_w = wide // 128

    def source(shape, axis):
        place = lax.broadcasted_iota(jnp.int32, shape, axis)
        block = lax.shift_right_logical(place, 7)
        spot = place - block * 128
        head = jnp.zeros(shape, jnp.int32)
        for number in range(1, heads + 1):
            head = head + jnp.where(spot >= number * per, 1, 0)
        dim = block * per + spot - head * per
        return jnp.where((head < heads) & (dim < DH), head * DH + dim, -1)

    row = lax.broadcasted_iota(jnp.int32, (width, wide), 0)
    perm[...] = jnp.where(row == source((1, wide), 1), 1.0, 0.0).astype(jnp.bfloat16)
    col = lax.broadcasted_iota(jnp.int32, (wide, width), 1)
    unperm[...] = jnp.where(col == source((wide, 1), 0), 1.0, 0.0).astype(jnp.bfloat16)

    def head_of(shape, axis):
        place = lax.broadcasted_iota(jnp.int32, shape, axis)
        head = jnp.where(place >= 128, heads + 1, 0)
        for number in range(1, heads + 1):
            head = head + jnp.where((place & 127) >= number * per, 1, 0)
        return jnp.where((place & 127) >= heads * per, -1 - axis, head)

    gather[...] = jnp.where(head_of((256, 1), 0) == head_of((1, 256), 1), 1.0 / DH**0.5, 0.0).astype(
        jnp.bfloat16
    )
    edge = jnp.zeros((pad, wide), jnp.float32)
    for buffer in (k_s, v_s):
        buffer[0:pad] = edge
        buffer[rows + pad : rows + 2 * pad] = edge
    for slot, plain, spread in ((8, wq, wqp), (9, wk, wkp), (10, wv, wvp)):
        stage[slot].wait()
        spread[...] = jnp.dot(
            plain[...], perm[...], preferred_element_type=jnp.float32
        ).astype(jnp.bfloat16)
    stage[11].wait()
    wop[...] = jnp.dot(unperm[...], wo[...], preferred_element_type=jnp.float32).astype(
        jnp.bfloat16
    )

    for slot in (3, 5, 6, 7):
        stage[slot].wait()
    for peer in peers:
        m_copy(peer, peer).wait_recv()
    facts = metas[...].reshape(n, 128)
    slot_index = lax.broadcasted_iota(jnp.int32, (n, 128), 0)
    bases = []
    for f in range(fdev):
        level = facts[:, f : f + 1]
        base = jnp.zeros((n, width), jnp.float32)
        speed = jnp.zeros((n, width), jnp.float32)
        for number in range(embed.shape[0]):
            chosen = level == number
            base = base + jnp.where(chosen, embed[number : number + 1, :], 0.0)
            speed = speed + jnp.where(chosen, srate_s[number], 0.0)
        bases.append(base)
        reach = jnp.broadcast_to(facts[:, fdev + f : fdev + f + 1], (n, 128))
        spot = slot_index * fdev + f
        for s in range(n):
            rate[s * fdev + f] = speed[s : s + 1]
        for slot in range(SPAN):
            offset = slot - BAND
            valid = jnp.where(
                (reach >= -offset) & (spot + offset >= 0) & (spot + offset < frames), 0.0, -1e30
            )
            for s in range(n):
                mask[slot, s * fdev + f] = valid[s : s + 1]

    for peer in peers:
        p_copy(peer, peer).wait_recv()
    pooled = jnp.sum(pool[...], axis=0) / float(text_tokens)
    pooled = jnp.broadcast_to(pooled, (16, pooled.shape[1])).astype(jnp.bfloat16)
    text = jnp.dot(pooled, proj[...], preferred_element_type=jnp.float32)[0:1]
    for f in range(fdev):
        full = bases[f] + text
        for s in range(n):
            cond[s * fdev + f] = full[s : s + 1]

    gain = gain_s[...].reshape(1, 1, width)
    cell = 8

    def project(current):
        hin = current + cond[...]
        power = jnp.mean(hin * hin, axis=-1, keepdims=True)
        flat = (hin * lax.rsqrt(power + 1e-06) * gain).reshape(rows, width).astype(jnp.bfloat16)
        q_s[...] = jnp.dot(flat, wqp[...], preferred_element_type=jnp.float32)
        k_s[pad : pad + rows] = jnp.dot(flat, wkp[...], preferred_element_type=jnp.float32)
        v_s[pad : pad + rows] = jnp.dot(flat, wvp[...], preferred_element_type=jnp.float32)

    def attend(current):
        size = cell * pos
        for first in range(0, frames, cell):
            start = first * pos
            for slot in range(SPAN):
                at = start + slot * pos
                total = None
                for block in range(blocks_w):
                    lanes = slice(block * 128, block * 128 + 128)
                    term = q_s[start : start + size, lanes] * k_s[at : at + size, lanes]
                    total = term if total is None else total + term
                part[start : start + size, slot * 128 : slot * 128 + 128] = total.astype(
                    jnp.bfloat16
                )
        raws = []
        for slot in range(0, SPAN, 2):
            lanes = min(2, SPAN - slot) * 128
            made = jnp.dot(
                part[:, slot * 128 : slot * 128 + lanes],
                gather[0:lanes, 0:lanes],
                preferred_element_type=jnp.float32,
            )
            raws.extend(made[:, at : at + 128] for at in range(0, lanes, 128))
        for first in range(0, frames, cell):
            start = first * pos
            scores = []
            for slot in range(SPAN):
                raw = raws[slot][start : start + size].reshape(cell, pos, 128)
                scores.append(raw + mask[slot, first : first + cell])
            top = functools.reduce(jnp.maximum, scores)
            expo = [jnp.exp(score - top) for score in scores]
            inverse = 1.0 / functools.reduce(jnp.add, expo)
            weights = [
                (one * inverse).reshape(size, 128).astype(jnp.bfloat16).astype(jnp.float32)
                for one in expo
            ]
            for block in range(blocks_w):
                lanes = slice(block * 128, block * 128 + 128)
                total = None
                for slot in range(SPAN):
                    at = start + slot * pos
                    term = weights[slot] * v_s[at : at + size, lanes]
                    total = term if total is None else total + term
                att[start : start + size, lanes] = total.astype(jnp.bfloat16)
        noise = jnp.dot(att[...], wop[...], preferred_element_type=jnp.float32)
        return current - rate[...] * noise.reshape(frames, pos, width)

    def half(h, carry):
        stage_x = pltpu.make_async_copy(x_hbm.at[:, me, h], recv.at[h, mine], local.at[12 + h])
        stage_x.wait()
        for peer in peers:
            x_copy(h, peer, peer).wait_recv()
        turn = fdev * pos
        for step in range(STEPS):
            last = step == STEPS - 1
            held = xa if step % 2 == 1 else xb
            fresh = xb if step % 2 == 1 else xa

            def load(first, count, step=step, held=held):
                if step == 0:
                    return recv[h, pl.ds(first, count)].astype(jnp.float32)
                start = pl.multiple_of(first * pos, 16)
                return (
                    held[pl.ds(start, count * pos)].astype(jnp.float32).reshape(count, pos, width)
                )

            project(load(0, frames))

            made = attend(load(0, frames))
            if last:
                xo[h] = made.astype(jnp.bfloat16)
            else:
                fresh[turn : turn + rows] = made.reshape(rows, width).astype(jnp.bfloat16)
            if not last:
                fresh[0:turn] = fresh[rows : rows + turn]
        for peer in peers:
            o_copy(h, lax.rem(peer + n - 1, n), me, peer).start()
        pltpu.make_async_copy(
            xo.at[h, pl.ds(lax.rem(me + n - 1, n) * fdev, fdev)],
            out_hbm.at[:, me, h],
            local.at[12 + halves + h],
        ).start()
        return carry

    lax.fori_loop(0, halves, half, 0)

    for h in range(halves):
        for peer in peers:
            x_copy(h, peer, me).wait_send()
    for peer in peers:
        m_copy(peer, me).wait_send()
        p_copy(peer, me).wait_send()
    for h in range(halves):
        pltpu.make_async_copy(
            xo.at[h, pl.ds(lax.rem(me + n - 1, n) * fdev, fdev)],
            out_hbm.at[:, me, h],
            local.at[12 + halves + h],
        ).wait()
        for peer in peers:
            o_copy(h, lax.rem(peer + n - 1, n), me, peer).wait_send()
            o_copy(h, lax.rem(me + n - 1, n), peer, me).wait_recv()


HALVES = 2
GRANT = 40 << 20


def fused(
    latents,
    levels,
    back_reach,
    text_ids,
    text_table,
    text_proj,
    level_embed,
    step_rate,
    norm_gain,
    w_query,
    w_key,
    w_value,
    w_out,
):
    n = lax.axis_size("level")
    fdev, tokens, width = latents.shape
    pos = tokens // (n * HALVES)
    frames = fdev * n
    rows = frames * pos
    bf16, f32, i32 = jnp.bfloat16, jnp.float32, jnp.int32
    anywhere = pl.BlockSpec(memory_space=pl.ANY)
    stored = pl.BlockSpec(memory_space=pltpu.HBM)
    dma = pltpu.SemaphoreType.DMA
    block = pltpu.VMEM((HALVES, frames, pos, width), bf16)
    rolled = pltpu.VMEM((rows + fdev * pos, width), bf16)
    wide = -(-DH // (128 // (width // DH))) * 128
    padded = pltpu.VMEM((rows + 2 * BAND * pos, wide), f32)
    square = pltpu.VMEM((width, width), bf16)
    out = pl.pallas_call(
        functools.partial(queue_kernel, n),
        out_shape=jax.ShapeDtypeStruct((fdev, n, HALVES, pos, width), bf16),
        in_specs=[stored] * 13,
        out_specs=anywhere,
        scratch_shapes=[
            block,
            rolled,
            rolled,
            block,
            pltpu.VMEM((rows, wide), f32),
            padded,
            padded,
            pltpu.VMEM((rows, SPAN * 128), bf16),
            pltpu.VMEM((rows, wide), bf16),
            pltpu.VMEM(text_table.shape, bf16),
            pltpu.VMEM(text_proj.shape, bf16),
            pltpu.VMEM(level_embed.shape, f32),
            pltpu.VMEM(norm_gain.shape, f32),
            square,
            square,
            square,
            square,
            pltpu.VMEM((width, wide), bf16),
            pltpu.VMEM((width, wide), bf16),
            pltpu.VMEM((width, wide), bf16),
            pltpu.VMEM((wide, width), bf16),
            pltpu.SMEM(levels.shape, i32),
            pltpu.SMEM(back_reach.shape, i32),
            pltpu.SMEM(text_ids.shape, i32),
            pltpu.SMEM(step_rate.shape, f32),
            pltpu.VMEM((n, 1, text_table.shape[1]), f32),
            pltpu.VMEM((n, 1, 128), i32),
            pltpu.VMEM((frames, 1, width), f32),
            pltpu.VMEM((frames, 1, width), f32),
            pltpu.VMEM((SPAN, frames, 1, 128), f32),
            pltpu.VMEM((width, wide), bf16),
            pltpu.VMEM((wide, width), bf16),
            pltpu.VMEM((256, 256), bf16),
            dma((HALVES, n)),
            dma((HALVES, n)),
            dma((n,)),
            dma((n,)),
            dma((n,)),
            dma((n,)),
            dma((HALVES, n)),
            dma((HALVES, n)),
            dma((12 + 2 * HALVES,)),
        ],
        compiler_params=pltpu.CompilerParams(
            collective_id=0, has_side_effects=True, vmem_limit_bytes=GRANT
        ),
        name="queue",
    )(
        *(
            pltpu.with_memory_space_constraint(value, pltpu.HBM)
            for value in (
                latents.reshape(fdev, n, HALVES, pos, width),
                levels,
                back_reach,
                text_ids,
                text_table,
                text_proj,
                level_embed,
                step_rate,
                norm_gain,
                w_query,
                w_key,
                w_value,
                w_out,
            )
        )
    )
    return out.reshape(fdev, tokens, width)


def general(
    latents,
    levels,
    back_reach,
    text_ids,
    text_table,
    text_proj,
    level_embed,
    step_rate,
    norm_gain,
    w_query,
    w_key,
    w_value,
    w_out,
):
    n = lax.axis_size("level")
    index = lax.axis_index("level")
    fdev, tokens, width = latents.shape
    heads = width // DH
    frames = fdev * n
    vocab = text_table.shape[0]
    spots = index * vocab + jnp.arange(vocab, dtype=jnp.int32)
    counts = jnp.sum((text_ids[:, None] == spots[None, :]).astype(jnp.float32), axis=0)
    partial = jnp.dot(
        counts.astype(jnp.bfloat16)[None, :], text_table, preferred_element_type=jnp.float32
    )
    pooled = lax.psum(partial, "level") / text_ids.shape[0]
    text_vec = jnp.dot(pooled.astype(jnp.bfloat16), text_proj, preferred_element_type=jnp.float32)
    levels = lax.all_gather(levels, "level", tiled=True)
    reach = lax.all_gather(back_reach, "level", tiled=True)
    cond = level_embed[levels] + text_vec
    rate = step_rate[levels]
    current = lax.all_to_all(latents, "level", split_axis=1, concat_axis=0, tiled=True)
    pos = tokens // n
    spot = jnp.arange(frames, dtype=jnp.int32)
    for step in range(STEPS):
        hin = current.astype(jnp.float32) + cond[:, None, :]
        power = jnp.mean(hin * hin, axis=-1, keepdims=True)
        normed = (hin * lax.rsqrt(power + 1e-06) * norm_gain).astype(jnp.bfloat16)
        flat = normed.reshape(-1, width)

        def project(weight):
            out = jnp.dot(flat, weight, preferred_element_type=jnp.float32)
            return out.astype(jnp.bfloat16).reshape(frames, pos, heads, DH).astype(jnp.float32)

        edge = ((BAND, BAND), (0, 0), (0, 0), (0, 0))
        query = project(w_query)
        keys = jnp.pad(project(w_key), edge)
        values = jnp.pad(project(w_value), edge)
        scores = []
        masks = []
        for offset in range(-BAND, BAND + 1):
            raw = jnp.sum(query * keys[BAND + offset : BAND + offset + frames], -1) / DH**0.5
            valid = (offset >= -reach) & (spot + offset >= 0) & (spot + offset < frames)
            scores.append(jnp.where(valid[:, None, None], raw, -1e30))
            masks.append(valid.astype(jnp.float32)[:, None, None])
        scores = jnp.stack(scores)
        expo = jnp.exp(scores - jnp.max(scores, axis=0)[None]) * jnp.stack(masks)
        weights = (expo / jnp.sum(expo, axis=0)[None]).astype(jnp.bfloat16).astype(jnp.float32)
        attended = jnp.zeros((frames, pos, heads, DH), jnp.float32)
        for slot in range(SPAN):
            attended = attended + weights[slot][..., None] * values[slot : slot + frames]
        noise = jnp.dot(
            attended.astype(jnp.bfloat16).reshape(-1, width),
            w_out,
            preferred_element_type=jnp.float32,
        ).reshape(frames, pos, width)
        updated = current.astype(jnp.float32) - rate[:, None, None] * noise
        current = jnp.roll(updated.astype(jnp.bfloat16), fdev, axis=0)
    return lax.all_to_all(current, "level", split_axis=0, concat_axis=1, tiled=True)


def per_device(latents, *rest):
    n = lax.axis_size("level")
    tokens = latents.shape[1]
    fits = tokens % (8 * HALVES * n) == 0 and latents.shape[0] * n % 8 == 0
    if fits and n & (n - 1) == 0:
        return fused(latents, *rest)
    return general(latents, *rest)


def solution(mesh):
    in_specs = (
        P(("groups", "level"), None, None),
        P(("groups", "level")),
        P(("groups", "level")),
        P("groups"),
        P("level", None),
        P(),
        P(),
        P(),
        P(),
        P(),
        P(),
        P(),
        P(),
    )
    out_specs = P(("groups", "level"), None, None)
    return jax.shard_map(
        per_device, mesh=mesh, in_specs=in_specs, out_specs=out_specs, check_vma=False
    )
```

```python
import functools

import jax
import jax.numpy as jnp
from jax import lax
from jax.experimental import pallas as pl
from jax.experimental.pallas import tpu as pltpu
from jax.sharding import PartitionSpec as P

DH = 64
BAND = 2
STEPS = 3
SPAN = 2 * BAND + 1
MESH = pl.DeviceIdType.MESH


def queue_kernel(
    n,
    x_hbm,
    level_hbm,
    reach_hbm,
    ids_hbm,
    table_hbm,
    proj_hbm,
    embed_hbm,
    srate_hbm,
    gain_hbm,
    wq_hbm,
    wk_hbm,
    wv_hbm,
    wo_hbm,
    out_hbm,
    recv,
    xa,
    xb,
    xo,
    q_s,
    k_s,
    v_s,
    part,
    att,
    table,
    proj,
    embed,
    gain_s,
    plain,
    wo,
    spread,
    wop,
    level_s,
    reach_s,
    ids_s,
    srate_s,
    pool,
    metas,
    metas_s,
    cond,
    rate,
    mask,
    perm,
    unperm,
    gather,
    x_send,
    x_recv,
    p_send,
    p_recv,
    m_send,
    m_recv,
    o_send,
    o_recv,
    local,
):
    me = lax.axis_index("level")
    fdev = x_hbm.shape[0]
    halves, frames, pos, width = recv.shape
    rows = frames * pos
    pad = BAND * pos
    barrier = pltpu.get_barrier_semaphore()
    for hop in range(1, n):
        pl.semaphore_signal(
            barrier, inc=1, device_id={"level": lax.rem(me + hop, n)}, device_id_type=MESH
        )
    mine = pl.ds(me * fdev, fdev)
    pairs = [
        (level_hbm, level_s),
        (reach_hbm, reach_s),
        (ids_hbm, ids_s),
        (srate_hbm, srate_s),
        (table_hbm, table),
        (embed_hbm, embed),
        (gain_hbm, gain_s),
        (proj_hbm, proj),
        (wq_hbm, plain.at[0]),
        (wk_hbm, plain.at[1]),
        (wv_hbm, plain.at[2]),
        (wo_hbm, wo),
    ] + [(x_hbm.at[:, me, h], recv.at[h, mine]) for h in range(halves)]
    stage = [
        pltpu.make_async_copy(src, dst, local.at[slot]) for slot, (src, dst) in enumerate(pairs)
    ]
    for copy in stage:
        copy.start()

    def x_copy(h, peer, owner):
        return pltpu.make_async_remote_copy(
            src_ref=x_hbm.at[:, peer, h],
            dst_ref=recv.at[h, pl.ds(owner * fdev, fdev)],
            send_sem=x_send.at[h, peer],
            recv_sem=x_recv.at[h, owner],
            device_id={"level": peer},
            device_id_type=MESH,
        )

    def p_copy(peer, owner):
        return pltpu.make_async_remote_copy(
            src_ref=pool.at[owner],
            dst_ref=pool.at[owner],
            send_sem=p_send.at[peer],
            recv_sem=p_recv.at[owner],
            device_id={"level": peer},
            device_id_type=MESH,
        )

    def m_copy(peer, owner):
        return pltpu.make_async_remote_copy(
            src_ref=metas.at[owner],
            dst_ref=metas.at[owner],
            send_sem=m_send.at[peer],
            recv_sem=m_recv.at[owner],
            device_id={"level": peer},
            device_id_type=MESH,
        )

    def o_copy(h, section, owner, peer):
        return pltpu.make_async_remote_copy(
            src_ref=xo.at[h, pl.ds(section * fdev, fdev)],
            dst_ref=out_hbm.at[:, owner, h],
            send_sem=o_send.at[h, peer],
            recv_sem=o_recv.at[h, owner],
            device_id={"level": peer},
            device_id_type=MESH,
        )

    def flip(bits):
        other = me
        for place in range(n.bit_length()):
            if bits >> place & 1:
                bit = lax.rem(lax.div(me, 1 << place), 2)
                other = other + (1 - 2 * bit) * (1 << place)
        return other

    first = [bits for bits in (8, 12, 9, 4, 1, 2, 5, 3) if bits < n]
    order = first + [bits for bits in range(n - 1, 0, -1) if bits not in first]
    peers = [flip(bits) for bits in order]
    pl.semaphore_wait(barrier, n - 1)
    early = len(first)
    for peer in peers[:early]:
        x_copy(0, peer, me).start()

    stage[0].wait()
    stage[1].wait()
    lane = lax.broadcasted_iota(jnp.int32, (1, 128), 1)
    fact = jnp.zeros((1, 128), jnp.int32)
    for f in range(fdev):
        fact = jnp.where(lane == f, level_s[f], fact)
        fact = jnp.where(lane == fdev + f, reach_s[f], fact)
    metas[me] = fact
    for peer in peers:
        m_copy(peer, me).start()

    vocab = table.shape[0]
    stage[2].wait()
    first_id = me * vocab
    text_tokens = ids_s.shape[0]
    sublane = lax.broadcasted_iota(jnp.int32, (8, 1), 0)
    spots = lax.broadcasted_iota(jnp.int32, (8, vocab), 1)
    counts = jnp.zeros((8, vocab), jnp.float32)
    for first_token in range(0, text_tokens, 8):
        wanted = jnp.full((8, 1), -1, jnp.int32)
        for token in range(first_token, min(first_token + 8, text_tokens)):
            wanted = jnp.where(sublane == token - first_token, ids_s[token] - first_id, wanted)
        counts = counts + jnp.where(spots == wanted, 1.0, 0.0)
    counts = jnp.concatenate([counts, jnp.zeros((8, vocab), jnp.float32)], axis=0).astype(
        jnp.bfloat16
    )
    stage[4].wait()
    partial = jnp.dot(counts, table[...], preferred_element_type=jnp.float32)
    pool[me] = jnp.sum(partial[0:8], axis=0, keepdims=True)
    for peer in peers:
        p_copy(peer, me).start()
    for peer in peers[early:]:
        x_copy(0, peer, me).start()
    for h in range(1, halves):
        for peer in peers:
            x_copy(h, peer, me).start()

    heads = width // DH
    per = 128 // heads
    wide = k_s.shape[1]
    blocks_w = wide // 128

    def source(place):
        block = lax.shift_right_logical(place, 7)
        spot = place - block * 128
        head = jnp.zeros(place.shape, jnp.int32)
        for number in range(1, heads + 1):
            head = head + jnp.where(spot >= number * per, 1, 0)
        dim = block * per + spot - head * per
        return jnp.where((head < heads) & (dim < DH), head * DH + dim, -1)

    strip = 64

    def build_perm(index, carry):
        at = pl.multiple_of(index * strip, strip)
        row = lax.broadcasted_iota(jnp.int32, (strip, wide), 0) + at
        here = row == source(lax.broadcasted_iota(jnp.int32, (1, wide), 1))
        perm[pl.ds(at, strip)] = jnp.where(here, 1.0, 0.0).astype(jnp.bfloat16)
        return carry

    def build_unperm(index, carry):
        at = pl.multiple_of(index * strip, strip)
        col = lax.broadcasted_iota(jnp.int32, (strip, width), 1)
        here = col == source(lax.broadcasted_iota(jnp.int32, (strip, 1), 0) + at)
        unperm[pl.ds(at, strip)] = jnp.where(here, 1.0, 0.0).astype(jnp.bfloat16)
        return carry

    lax.fori_loop(0, width // strip, build_perm, 0)
    lax.fori_loop(0, wide // strip, build_unperm, 0)

    def head_of(shape, axis):
        place = lax.broadcasted_iota(jnp.int32, shape, axis)
        head = jnp.where(place >= 128, heads + 1, 0)
        for number in range(1, heads + 1):
            head = head + jnp.where((place & 127) >= number * per, 1, 0)
        return jnp.where((place & 127) >= heads * per, -1 - axis, head)

    gather[...] = jnp.where(head_of((256, 1), 0) == head_of((1, 256), 1), 1.0 / DH**0.5, 0.0).astype(
        jnp.bfloat16
    )
    edge = jnp.zeros((pad, wide), jnp.float32)
    for buffer in (k_s, v_s):
        buffer[0:pad] = edge
        buffer[rows + pad : rows + 2 * pad] = edge
    for peer in peers:
        m_copy(peer, peer).wait_recv()
    told = pltpu.make_async_copy(metas, metas_s, local.at[12 + 2 * halves])
    told.start()
    for slot in (8, 9, 10, 11):
        stage[slot].wait()

    def respread(index, carry):
        spread[index] = jnp.dot(
            plain[index], perm[...], preferred_element_type=jnp.float32
        ).astype(jnp.bfloat16)
        return carry

    lax.fori_loop(0, 3, respread, 0)
    wop[...] = jnp.dot(unperm[...], wo[...], preferred_element_type=jnp.float32).astype(
        jnp.bfloat16
    )

    for slot in (3, 5, 6, 7):
        stage[slot].wait()
    told.wait()
    for frame in range(frames):
        s, f = divmod(frame, fdev)
        level = metas_s[s, 0, f]
        reach = metas_s[s, 0, fdev + f]
        rate[frame] = jnp.full((1, width), srate_s[level], jnp.float32)
        cond[frame] = embed[pl.ds(level, 1), :]
        for slot in range(SPAN):
            offset = slot - BAND
            inside = 0 <= frame + offset < frames
            if offset < 0 and inside:
                value = jnp.where(reach >= -offset, 0.0, -1e30)
            else:
                value = 0.0 if inside else -1e30
            mask[slot, frame] = jnp.full((1, 128), value, jnp.float32)

    for peer in peers:
        p_copy(peer, peer).wait_recv()
    pooled = jnp.sum(pool[...], axis=0) / float(text_tokens)
    pooled = jnp.broadcast_to(pooled, (16, pooled.shape[1])).astype(jnp.bfloat16)
    text = jnp.dot(pooled, proj[...], preferred_element_type=jnp.float32)[0:1]
    cond[...] = cond[...] + text.reshape(1, 1, width)

    gain = gain_s[...].reshape(1, 1, width)
    cell = 8

    def project(current):
        hin = current + cond[...]
        power = jnp.mean(hin * hin, axis=-1, keepdims=True)
        flat = (hin * lax.rsqrt(power + 1e-06) * gain).reshape(rows, width).astype(jnp.bfloat16)
        q_s[...] = jnp.dot(flat, spread[0], preferred_element_type=jnp.float32)
        k_s[pad : pad + rows] = jnp.dot(flat, spread[1], preferred_element_type=jnp.float32)
        v_s[pad : pad + rows] = jnp.dot(flat, spread[2], preferred_element_type=jnp.float32)

    def attend(current):
        size = cell * pos
        for first in range(0, frames, cell):
            start = first * pos
            for slot in range(SPAN):
                at = start + slot * pos
                total = None
                for block in range(blocks_w):
                    lanes = slice(block * 128, block * 128 + 128)
                    term = q_s[start : start + size, lanes] * k_s[at : at + size, lanes]
                    total = term if total is None else total + term
                part[start : start + size, slot * 128 : slot * 128 + 128] = total.astype(
                    jnp.bfloat16
                )
        raws = []
        for slot in range(0, SPAN, 2):
            lanes = min(2, SPAN - slot) * 128
            made = jnp.dot(
                part[:, slot * 128 : slot * 128 + lanes],
                gather[0:lanes, 0:lanes],
                preferred_element_type=jnp.float32,
            )
            raws.extend(made[:, at : at + 128] for at in range(0, lanes, 128))
        for first in range(0, frames, cell):
            start = first * pos
            scores = []
            for slot in range(SPAN):
                raw = raws[slot][start : start + size].reshape(cell, pos, 128)
                scores.append(raw + mask[slot, first : first + cell])
            top = functools.reduce(jnp.maximum, scores)
            expo = [jnp.exp(score - top) for score in scores]
            inverse = 1.0 / functools.reduce(jnp.add, expo)
            weights = [
                (one * inverse).reshape(size, 128).astype(jnp.bfloat16).astype(jnp.float32)
                for one in expo
            ]
            for block in range(blocks_w):
                lanes = slice(block * 128, block * 128 + 128)
                total = None
                for slot in range(SPAN):
                    at = start + slot * pos
                    term = weights[slot] * v_s[at : at + size, lanes]
                    total = term if total is None else total + term
                att[start : start + size, lanes] = total.astype(jnp.bfloat16)
        noise = jnp.dot(att[...], wop[...], preferred_element_type=jnp.float32)
        return current - rate[...] * noise.reshape(frames, pos, width)

    def half(h, carry):
        stage_x = pltpu.make_async_copy(x_hbm.at[:, me, h], recv.at[h, mine], local.at[12 + h])
        stage_x.wait()
        for peer in peers:
            x_copy(h, peer, peer).wait_recv()
        turn = fdev * pos
        for step in range(STEPS):
            last = step == STEPS - 1
            held = xa if step % 2 == 1 else xb
            fresh = xb if step % 2 == 1 else xa

            def load(first, count, step=step, held=held):
                if step == 0:
                    return recv[h, pl.ds(first, count)].astype(jnp.float32)
                start = pl.multiple_of(first * pos, 16)
                return (
                    held[pl.ds(start, count * pos)].astype(jnp.float32).reshape(count, pos, width)
                )

            project(load(0, frames))

            made = attend(load(0, frames))
            if last:
                xo[h] = made.astype(jnp.bfloat16)
            else:
                fresh[turn : turn + rows] = made.reshape(rows, width).astype(jnp.bfloat16)
            if not last:
                fresh[0:turn] = fresh[rows : rows + turn]
        for peer in peers:
            o_copy(h, lax.rem(peer + n - 1, n), me, peer).start()
        pltpu.make_async_copy(
            xo.at[h, pl.ds(lax.rem(me + n - 1, n) * fdev, fdev)],
            out_hbm.at[:, me, h],
            local.at[12 + halves + h],
        ).start()
        return carry

    lax.fori_loop(0, halves, half, 0)

    for h in range(halves):
        for peer in peers:
            x_copy(h, peer, me).wait_send()
    for peer in peers:
        m_copy(peer, me).wait_send()
        p_copy(peer, me).wait_send()
    for h in range(halves):
        pltpu.make_async_copy(
            xo.at[h, pl.ds(lax.rem(me + n - 1, n) * fdev, fdev)],
            out_hbm.at[:, me, h],
            local.at[12 + halves + h],
        ).wait()
        for peer in peers:
            o_copy(h, lax.rem(peer + n - 1, n), me, peer).wait_send()
            o_copy(h, lax.rem(me + n - 1, n), peer, me).wait_recv()


HALVES = 2
GRANT = 40 << 20


def fused(
    latents,
    levels,
    back_reach,
    text_ids,
    text_table,
    text_proj,
    level_embed,
    step_rate,
    norm_gain,
    w_query,
    w_key,
    w_value,
    w_out,
):
    n = lax.axis_size("level")
    fdev, tokens, width = latents.shape
    pos = tokens // (n * HALVES)
    frames = fdev * n
    rows = frames * pos
    bf16, f32, i32 = jnp.bfloat16, jnp.float32, jnp.int32
    anywhere = pl.BlockSpec(memory_space=pl.ANY)
    stored = pl.BlockSpec(memory_space=pltpu.HBM)
    dma = pltpu.SemaphoreType.DMA
    block = pltpu.VMEM((HALVES, frames, pos, width), bf16)
    rolled = pltpu.VMEM((rows + fdev * pos, width), bf16)
    wide = -(-DH // (128 // (width // DH))) * 128
    padded = pltpu.VMEM((rows + 2 * BAND * pos, wide), f32)
    square = pltpu.VMEM((width, width), bf16)
    out = pl.pallas_call(
        functools.partial(queue_kernel, n),
        out_shape=jax.ShapeDtypeStruct((fdev, n, HALVES, pos, width), bf16),
        in_specs=[stored] * 13,
        out_specs=anywhere,
        scratch_shapes=[
            block,
            rolled,
            rolled,
            block,
            pltpu.VMEM((rows, wide), f32),
            padded,
            padded,
            pltpu.VMEM((rows, SPAN * 128), bf16),
            pltpu.VMEM((rows, wide), bf16),
            pltpu.VMEM(text_table.shape, bf16),
            pltpu.VMEM(text_proj.shape, bf16),
            pltpu.VMEM(level_embed.shape, f32),
            pltpu.VMEM(norm_gain.shape, f32),
            pltpu.VMEM((3, width, width), bf16),
            square,
            pltpu.VMEM((3, width, wide), bf16),
            pltpu.VMEM((wide, width), bf16),
            pltpu.SMEM(levels.shape, i32),
            pltpu.SMEM(back_reach.shape, i32),
            pltpu.SMEM(text_ids.shape, i32),
            pltpu.SMEM(step_rate.shape, f32),
            pltpu.VMEM((n, 1, text_table.shape[1]), f32),
            pltpu.VMEM((n, 1, 128), i32),
            pltpu.SMEM((n, 1, 128), i32),
            pltpu.VMEM((frames, 1, width), f32),
            pltpu.VMEM((frames, 1, width), f32),
            pltpu.VMEM((SPAN, frames, 1, 128), f32),
            pltpu.VMEM((width, wide), bf16),
            pltpu.VMEM((wide, width), bf16),
            pltpu.VMEM((256, 256), bf16),
            dma((HALVES, n)),
            dma((HALVES, n)),
            dma((n,)),
            dma((n,)),
            dma((n,)),
            dma((n,)),
            dma((HALVES, n)),
            dma((HALVES, n)),
            dma((13 + 2 * HALVES,)),
        ],
        compiler_params=pltpu.CompilerParams(
            collective_id=0, has_side_effects=True, vmem_limit_bytes=GRANT
        ),
        name="queue",
    )(
        *(
            pltpu.with_memory_space_constraint(value, pltpu.HBM)
            for value in (
                latents.reshape(fdev, n, HALVES, pos, width),
                levels,
                back_reach,
                text_ids,
                text_table,
                text_proj,
                level_embed,
                step_rate,
                norm_gain,
                w_query,
                w_key,
                w_value,
                w_out,
            )
        )
    )
    return out.reshape(fdev, tokens, width)


def general(
    latents,
    levels,
    back_reach,
    text_ids,
    text_table,
    text_proj,
    level_embed,
    step_rate,
    norm_gain,
    w_query,
    w_key,
    w_value,
    w_out,
):
    n = lax.axis_size("level")
    index = lax.axis_index("level")
    fdev, tokens, width = latents.shape
    heads = width // DH
    frames = fdev * n
    vocab = text_table.shape[0]
    spots = index * vocab + jnp.arange(vocab, dtype=jnp.int32)
    counts = jnp.sum((text_ids[:, None] == spots[None, :]).astype(jnp.float32), axis=0)
    partial = jnp.dot(
        counts.astype(jnp.bfloat16)[None, :], text_table, preferred_element_type=jnp.float32
    )
    pooled = lax.psum(partial, "level") / text_ids.shape[0]
    text_vec = jnp.dot(pooled.astype(jnp.bfloat16), text_proj, preferred_element_type=jnp.float32)
    levels = lax.all_gather(levels, "level", tiled=True)
    reach = lax.all_gather(back_reach, "level", tiled=True)
    cond = level_embed[levels] + text_vec
    rate = step_rate[levels]
    current = lax.all_to_all(latents, "level", split_axis=1, concat_axis=0, tiled=True)
    pos = tokens // n
    spot = jnp.arange(frames, dtype=jnp.int32)
    for step in range(STEPS):
        hin = current.astype(jnp.float32) + cond[:, None, :]
        power = jnp.mean(hin * hin, axis=-1, keepdims=True)
        normed = (hin * lax.rsqrt(power + 1e-06) * norm_gain).astype(jnp.bfloat16)
        flat = normed.reshape(-1, width)

        def project(weight):
            out = jnp.dot(flat, weight, preferred_element_type=jnp.float32)
            return out.astype(jnp.bfloat16).reshape(frames, pos, heads, DH).astype(jnp.float32)

        edge = ((BAND, BAND), (0, 0), (0, 0), (0, 0))
        query = project(w_query)
        keys = jnp.pad(project(w_key), edge)
        values = jnp.pad(project(w_value), edge)
        scores = []
        masks = []
        for offset in range(-BAND, BAND + 1):
            raw = jnp.sum(query * keys[BAND + offset : BAND + offset + frames], -1) / DH**0.5
            valid = (offset >= -reach) & (spot + offset >= 0) & (spot + offset < frames)
            scores.append(jnp.where(valid[:, None, None], raw, -1e30))
            masks.append(valid.astype(jnp.float32)[:, None, None])
        scores = jnp.stack(scores)
        expo = jnp.exp(scores - jnp.max(scores, axis=0)[None]) * jnp.stack(masks)
        weights = (expo / jnp.sum(expo, axis=0)[None]).astype(jnp.bfloat16).astype(jnp.float32)
        attended = jnp.zeros((frames, pos, heads, DH), jnp.float32)
        for slot in range(SPAN):
            attended = attended + weights[slot][..., None] * values[slot : slot + frames]
        noise = jnp.dot(
            attended.astype(jnp.bfloat16).reshape(-1, width),
            w_out,
            preferred_element_type=jnp.float32,
        ).reshape(frames, pos, width)
        updated = current.astype(jnp.float32) - rate[:, None, None] * noise
        current = jnp.roll(updated.astype(jnp.bfloat16), fdev, axis=0)
    return lax.all_to_all(current, "level", split_axis=0, concat_axis=1, tiled=True)


def per_device(latents, *rest):
    n = lax.axis_size("level")
    tokens = latents.shape[1]
    fits = tokens % (8 * HALVES * n) == 0 and latents.shape[0] * n % 8 == 0
    if fits and n & (n - 1) == 0:
        return fused(latents, *rest)
    return general(latents, *rest)


def solution(mesh):
    in_specs = (
        P(("groups", "level"), None, None),
        P(("groups", "level")),
        P(("groups", "level")),
        P("groups"),
        P("level", None),
        P(),
        P(),
        P(),
        P(),
        P(),
        P(),
        P(),
        P(),
    )
    out_specs = P(("groups", "level"), None, None)
    return jax.shard_map(
        per_device, mesh=mesh, in_specs=in_specs, out_specs=out_specs, check_vma=False
    )
```

```python
import functools

import jax
import jax.numpy as jnp
from jax import lax
from jax.experimental import pallas as pl
from jax.experimental.pallas import tpu as pltpu
from jax.sharding import PartitionSpec as P

DH = 64
BAND = 2
STEPS = 3
SPAN = 2 * BAND + 1
MESH = pl.DeviceIdType.MESH


def queue_kernel(
    n,
    x_hbm,
    level_hbm,
    reach_hbm,
    ids_hbm,
    table_hbm,
    proj_hbm,
    embed_hbm,
    srate_hbm,
    gain_hbm,
    wq_hbm,
    wk_hbm,
    wv_hbm,
    wo_hbm,
    out_hbm,
    recv,
    xa,
    xb,
    xo,
    q_s,
    k_s,
    v_s,
    part,
    att,
    table,
    proj,
    embed,
    gain_s,
    plain,
    wo,
    spread,
    wop,
    level_s,
    reach_s,
    ids_s,
    srate_s,
    pool,
    metas,
    metas_s,
    cond,
    rate,
    mask,
    perm,
    unperm,
    gather,
    x_send,
    x_recv,
    p_send,
    p_recv,
    m_send,
    m_recv,
    o_send,
    o_recv,
    local,
):
    me = lax.axis_index("level")
    fdev = x_hbm.shape[0]
    halves, frames, pos, width = recv.shape
    rows = frames * pos
    pad = BAND * pos
    barrier = pltpu.get_barrier_semaphore()
    for hop in range(1, n):
        pl.semaphore_signal(
            barrier, inc=1, device_id={"level": lax.rem(me + hop, n)}, device_id_type=MESH
        )
    mine = pl.ds(me * fdev, fdev)
    pairs = [
        (level_hbm, level_s),
        (reach_hbm, reach_s),
        (ids_hbm, ids_s),
        (srate_hbm, srate_s),
        (table_hbm, table),
        (embed_hbm, embed),
        (gain_hbm, gain_s),
        (proj_hbm, proj),
        (wq_hbm, plain.at[0]),
        (wk_hbm, plain.at[1]),
        (wv_hbm, plain.at[2]),
        (wo_hbm, wo),
    ] + [(x_hbm.at[:, me, h], recv.at[h, mine]) for h in range(halves)]
    stage = [
        pltpu.make_async_copy(src, dst, local.at[slot]) for slot, (src, dst) in enumerate(pairs)
    ]
    for copy in stage:
        copy.start()

    def x_copy(h, peer, owner):
        return pltpu.make_async_remote_copy(
            src_ref=x_hbm.at[:, peer, h],
            dst_ref=recv.at[h, pl.ds(owner * fdev, fdev)],
            send_sem=x_send.at[h, peer],
            recv_sem=x_recv.at[h, owner],
            device_id={"level": peer},
            device_id_type=MESH,
        )

    def p_copy(peer, owner):
        return pltpu.make_async_remote_copy(
            src_ref=pool.at[owner],
            dst_ref=pool.at[owner],
            send_sem=p_send.at[peer],
            recv_sem=p_recv.at[owner],
            device_id={"level": peer},
            device_id_type=MESH,
        )

    def m_copy(peer, owner):
        return pltpu.make_async_remote_copy(
            src_ref=metas.at[owner],
            dst_ref=metas.at[owner],
            send_sem=m_send.at[peer],
            recv_sem=m_recv.at[owner],
            device_id={"level": peer},
            device_id_type=MESH,
        )

    def o_copy(h, section, owner, peer):
        return pltpu.make_async_remote_copy(
            src_ref=xo.at[h, pl.ds(section * fdev, fdev)],
            dst_ref=out_hbm.at[:, owner, h],
            send_sem=o_send.at[h, peer],
            recv_sem=o_recv.at[h, owner],
            device_id={"level": peer},
            device_id_type=MESH,
        )

    def flip(bits):
        other = me
        for place in range(n.bit_length()):
            if bits >> place & 1:
                bit = lax.rem(lax.div(me, 1 << place), 2)
                other = other + (1 - 2 * bit) * (1 << place)
        return other

    order = sorted(range(1, n), key=lambda bits: (bits < 4, not bits & 2, bits))
    peers = [flip(bits) for bits in order]
    pl.semaphore_wait(barrier, n - 1)
    early = 4
    for peer in peers[:early]:
        x_copy(0, peer, me).start()

    stage[0].wait()
    stage[1].wait()
    lane = lax.broadcasted_iota(jnp.int32, (1, 128), 1)
    fact = jnp.zeros((1, 128), jnp.int32)
    for f in range(fdev):
        fact = jnp.where(lane == f, level_s[f], fact)
        fact = jnp.where(lane == fdev + f, reach_s[f], fact)
    metas[me] = fact
    for peer in peers:
        m_copy(peer, me).start()

    vocab = table.shape[0]
    stage[2].wait()
    first_id = me * vocab
    text_tokens = ids_s.shape[0]
    sublane = lax.broadcasted_iota(jnp.int32, (8, 1), 0)
    spots = lax.broadcasted_iota(jnp.int32, (8, vocab), 1)
    counts = jnp.zeros((8, vocab), jnp.float32)
    for first_token in range(0, text_tokens, 8):
        wanted = jnp.full((8, 1), -1, jnp.int32)
        for token in range(first_token, min(first_token + 8, text_tokens)):
            wanted = jnp.where(sublane == token - first_token, ids_s[token] - first_id, wanted)
        counts = counts + jnp.where(spots == wanted, 1.0, 0.0)
    counts = jnp.concatenate([counts, jnp.zeros((8, vocab), jnp.float32)], axis=0).astype(
        jnp.bfloat16
    )
    stage[4].wait()
    partial = jnp.dot(counts, table[...], preferred_element_type=jnp.float32)
    pool[me] = jnp.sum(partial[0:8], axis=0, keepdims=True)
    for peer in peers:
        p_copy(peer, me).start()
    for peer in peers[early:]:
        x_copy(0, peer, me).start()
    for h in range(1, halves):
        for peer in peers:
            x_copy(h, peer, me).start()

    heads = width // DH
    per = 128 // heads
    wide = k_s.shape[1]
    blocks_w = wide // 128

    def source(place):
        block = lax.shift_right_logical(place, 7)
        spot = place - block * 128
        head = jnp.zeros(place.shape, jnp.int32)
        for number in range(1, heads + 1):
            head = head + jnp.where(spot >= number * per, 1, 0)
        dim = block * per + spot - head * per
        return jnp.where((head < heads) & (dim < DH), head * DH + dim, -1)

    strip = 64

    def build_perm(index, carry):
        at = pl.multiple_of(index * strip, strip)
        row = lax.broadcasted_iota(jnp.int32, (strip, wide), 0) + at
        here = row == source(lax.broadcasted_iota(jnp.int32, (1, wide), 1))
        perm[pl.ds(at, strip)] = jnp.where(here, 1.0, 0.0).astype(jnp.bfloat16)
        return carry

    def build_unperm(index, carry):
        at = pl.multiple_of(index * strip, strip)
        col = lax.broadcasted_iota(jnp.int32, (strip, width), 1)
        here = col == source(lax.broadcasted_iota(jnp.int32, (strip, 1), 0) + at)
        unperm[pl.ds(at, strip)] = jnp.where(here, 1.0, 0.0).astype(jnp.bfloat16)
        return carry

    lax.fori_loop(0, width // strip, build_perm, 0)
    lax.fori_loop(0, wide // strip, build_unperm, 0)

    def head_of(shape, axis):
        place = lax.broadcasted_iota(jnp.int32, shape, axis)
        head = jnp.where(place >= 128, heads + 1, 0)
        for number in range(1, heads + 1):
            head = head + jnp.where((place & 127) >= number * per, 1, 0)
        return jnp.where((place & 127) >= heads * per, -1 - axis, head)

    gather[...] = jnp.where(head_of((256, 1), 0) == head_of((1, 256), 1), 1.0 / DH**0.5, 0.0).astype(
        jnp.bfloat16
    )
    edge = jnp.zeros((pad, wide), jnp.float32)
    for buffer in (k_s, v_s):
        buffer[0:pad] = edge
        buffer[rows + pad : rows + 2 * pad] = edge
    for slot in (8, 9, 10, 11):
        stage[slot].wait()

    def respread(index, carry):
        spread[index] = jnp.dot(
            plain[index], perm[...], preferred_element_type=jnp.float32
        ).astype(jnp.bfloat16)
        return carry

    lax.fori_loop(0, 3, respread, 0)
    wop[...] = jnp.dot(unperm[...], wo[...], preferred_element_type=jnp.float32).astype(
        jnp.bfloat16
    )

    for peer in peers:
        m_copy(peer, peer).wait_recv()
    told = pltpu.make_async_copy(metas, metas_s, local.at[12 + 2 * halves])
    told.start()
    for slot in (3, 5, 6, 7):
        stage[slot].wait()
    told.wait()
    for frame in range(frames):
        s, f = divmod(frame, fdev)
        level = metas_s[s, 0, f]
        reach = metas_s[s, 0, fdev + f]
        rate[frame] = jnp.full((1, width), srate_s[level], jnp.float32)
        cond[frame] = embed[pl.ds(level, 1), :]
        for slot in range(SPAN):
            offset = slot - BAND
            inside = 0 <= frame + offset < frames
            if offset < 0 and inside:
                value = jnp.where(reach >= -offset, 0.0, -1e30)
            else:
                value = 0.0 if inside else -1e30
            mask[slot, frame] = jnp.full((1, 128), value, jnp.float32)

    for peer in peers:
        p_copy(peer, peer).wait_recv()
    pooled = jnp.sum(pool[...], axis=0) / float(text_tokens)
    pooled = jnp.broadcast_to(pooled, (16, pooled.shape[1])).astype(jnp.bfloat16)
    text = jnp.dot(pooled, proj[...], preferred_element_type=jnp.float32)[0:1]
    cond[...] = cond[...] + text.reshape(1, 1, width)

    gain = gain_s[...].reshape(1, 1, width)
    cell = 8

    def project(current):
        hin = current + cond[...]
        power = jnp.mean(hin * hin, axis=-1, keepdims=True)
        flat = (hin * lax.rsqrt(power + 1e-06) * gain).reshape(rows, width).astype(jnp.bfloat16)
        q_s[...] = jnp.dot(flat, spread[0], preferred_element_type=jnp.float32)
        k_s[pad : pad + rows] = jnp.dot(flat, spread[1], preferred_element_type=jnp.float32)
        v_s[pad : pad + rows] = jnp.dot(flat, spread[2], preferred_element_type=jnp.float32)

    def attend(current):
        size = cell * pos
        for first in range(0, frames, cell):
            start = first * pos
            for slot in range(SPAN):
                at = start + slot * pos
                total = None
                for block in range(blocks_w):
                    lanes = slice(block * 128, block * 128 + 128)
                    term = q_s[start : start + size, lanes] * k_s[at : at + size, lanes]
                    total = term if total is None else total + term
                part[start : start + size, slot * 128 : slot * 128 + 128] = total.astype(
                    jnp.bfloat16
                )
        raws = []
        for slot in range(0, SPAN, 2):
            lanes = min(2, SPAN - slot) * 128
            made = jnp.dot(
                part[:, slot * 128 : slot * 128 + lanes],
                gather[0:lanes, 0:lanes],
                preferred_element_type=jnp.float32,
            )
            raws.extend(made[:, at : at + 128] for at in range(0, lanes, 128))
        for first in range(0, frames, cell):
            start = first * pos
            scores = []
            for slot in range(SPAN):
                raw = raws[slot][start : start + size].reshape(cell, pos, 128)
                scores.append(raw + mask[slot, first : first + cell])
            top = functools.reduce(jnp.maximum, scores)
            expo = [jnp.exp(score - top) for score in scores]
            inverse = 1.0 / functools.reduce(jnp.add, expo)
            weights = [
                (one * inverse).reshape(size, 128).astype(jnp.bfloat16).astype(jnp.float32)
                for one in expo
            ]
            for block in range(blocks_w):
                lanes = slice(block * 128, block * 128 + 128)
                total = None
                for slot in range(SPAN):
                    at = start + slot * pos
                    term = weights[slot] * v_s[at : at + size, lanes]
                    total = term if total is None else total + term
                att[start : start + size, lanes] = total.astype(jnp.bfloat16)
        noise = jnp.dot(att[...], wop[...], preferred_element_type=jnp.float32)
        return current - rate[...] * noise.reshape(frames, pos, width)

    def half(h, carry):
        stage_x = pltpu.make_async_copy(x_hbm.at[:, me, h], recv.at[h, mine], local.at[12 + h])
        stage_x.wait()
        for peer in peers:
            x_copy(h, peer, peer).wait_recv()
        turn = fdev * pos
        for step in range(STEPS):
            last = step == STEPS - 1
            held = xa if step % 2 == 1 else xb
            fresh = xb if step % 2 == 1 else xa

            def load(first, count, step=step, held=held):
                if step == 0:
                    return recv[h, pl.ds(first, count)].astype(jnp.float32)
                start = pl.multiple_of(first * pos, 16)
                return (
                    held[pl.ds(start, count * pos)].astype(jnp.float32).reshape(count, pos, width)
                )

            project(load(0, frames))

            made = attend(load(0, frames))
            if last:
                xo[h] = made.astype(jnp.bfloat16)
            else:
                fresh[turn : turn + rows] = made.reshape(rows, width).astype(jnp.bfloat16)
            if not last:
                fresh[0:turn] = fresh[rows : rows + turn]
        for peer in peers:
            o_copy(h, lax.rem(peer + n - 1, n), me, peer).start()
        pltpu.make_async_copy(
            xo.at[h, pl.ds(lax.rem(me + n - 1, n) * fdev, fdev)],
            out_hbm.at[:, me, h],
            local.at[12 + halves + h],
        ).start()
        return carry

    lax.fori_loop(0, halves, half, 0)

    for h in range(halves):
        for peer in peers:
            x_copy(h, peer, me).wait_send()
    for peer in peers:
        m_copy(peer, me).wait_send()
        p_copy(peer, me).wait_send()
    for h in range(halves):
        pltpu.make_async_copy(
            xo.at[h, pl.ds(lax.rem(me + n - 1, n) * fdev, fdev)],
            out_hbm.at[:, me, h],
            local.at[12 + halves + h],
        ).wait()
        for peer in peers:
            o_copy(h, lax.rem(peer + n - 1, n), me, peer).wait_send()
            o_copy(h, lax.rem(me + n - 1, n), peer, me).wait_recv()


HALVES = 2
GRANT = 40 << 20


def fused(
    latents,
    levels,
    back_reach,
    text_ids,
    text_table,
    text_proj,
    level_embed,
    step_rate,
    norm_gain,
    w_query,
    w_key,
    w_value,
    w_out,
):
    n = lax.axis_size("level")
    fdev, tokens, width = latents.shape
    pos = tokens // (n * HALVES)
    frames = fdev * n
    rows = frames * pos
    bf16, f32, i32 = jnp.bfloat16, jnp.float32, jnp.int32
    anywhere = pl.BlockSpec(memory_space=pl.ANY)
    stored = pl.BlockSpec(memory_space=pltpu.HBM)
    dma = pltpu.SemaphoreType.DMA
    block = pltpu.VMEM((HALVES, frames, pos, width), bf16)
    rolled = pltpu.VMEM((rows + fdev * pos, width), bf16)
    wide = -(-DH // (128 // (width // DH))) * 128
    padded = pltpu.VMEM((rows + 2 * BAND * pos, wide), f32)
    square = pltpu.VMEM((width, width), bf16)
    out = pl.pallas_call(
        functools.partial(queue_kernel, n),
        out_shape=jax.ShapeDtypeStruct((fdev, n, HALVES, pos, width), bf16),
        in_specs=[stored] * 13,
        out_specs=anywhere,
        scratch_shapes=[
            block,
            rolled,
            rolled,
            block,
            pltpu.VMEM((rows, wide), f32),
            padded,
            padded,
            pltpu.VMEM((rows, SPAN * 128), bf16),
            pltpu.VMEM((rows, wide), bf16),
            pltpu.VMEM(text_table.shape, bf16),
            pltpu.VMEM(text_proj.shape, bf16),
            pltpu.VMEM(level_embed.shape, f32),
            pltpu.VMEM(norm_gain.shape, f32),
            pltpu.VMEM((3, width, width), bf16),
            square,
            pltpu.VMEM((3, width, wide), bf16),
            pltpu.VMEM((wide, width), bf16),
            pltpu.SMEM(levels.shape, i32),
            pltpu.SMEM(back_reach.shape, i32),
            pltpu.SMEM(text_ids.shape, i32),
            pltpu.SMEM(step_rate.shape, f32),
            pltpu.VMEM((n, 1, text_table.shape[1]), f32),
            pltpu.VMEM((n, 1, 128), i32),
            pltpu.SMEM((n, 1, 128), i32),
            pltpu.VMEM((frames, 1, width), f32),
            pltpu.VMEM((frames, 1, width), f32),
            pltpu.VMEM((SPAN, frames, 1, 128), f32),
            pltpu.VMEM((width, wide), bf16),
            pltpu.VMEM((wide, width), bf16),
            pltpu.VMEM((256, 256), bf16),
            dma((HALVES, n)),
            dma((HALVES, n)),
            dma((n,)),
            dma((n,)),
            dma((n,)),
            dma((n,)),
            dma((HALVES, n)),
            dma((HALVES, n)),
            dma((13 + 2 * HALVES,)),
        ],
        compiler_params=pltpu.CompilerParams(
            collective_id=0, has_side_effects=True, vmem_limit_bytes=GRANT
        ),
        name="queue",
    )(
        *(
            pltpu.with_memory_space_constraint(value, pltpu.HBM)
            for value in (
                latents.reshape(fdev, n, HALVES, pos, width),
                levels,
                back_reach,
                text_ids,
                text_table,
                text_proj,
                level_embed,
                step_rate,
                norm_gain,
                w_query,
                w_key,
                w_value,
                w_out,
            )
        )
    )
    return out.reshape(fdev, tokens, width)


def general(
    latents,
    levels,
    back_reach,
    text_ids,
    text_table,
    text_proj,
    level_embed,
    step_rate,
    norm_gain,
    w_query,
    w_key,
    w_value,
    w_out,
):
    n = lax.axis_size("level")
    index = lax.axis_index("level")
    fdev, tokens, width = latents.shape
    heads = width // DH
    frames = fdev * n
    vocab = text_table.shape[0]
    spots = index * vocab + jnp.arange(vocab, dtype=jnp.int32)
    counts = jnp.sum((text_ids[:, None] == spots[None, :]).astype(jnp.float32), axis=0)
    partial = jnp.dot(
        counts.astype(jnp.bfloat16)[None, :], text_table, preferred_element_type=jnp.float32
    )
    pooled = lax.psum(partial, "level") / text_ids.shape[0]
    text_vec = jnp.dot(pooled.astype(jnp.bfloat16), text_proj, preferred_element_type=jnp.float32)
    levels = lax.all_gather(levels, "level", tiled=True)
    reach = lax.all_gather(back_reach, "level", tiled=True)
    cond = level_embed[levels] + text_vec
    rate = step_rate[levels]
    current = lax.all_to_all(latents, "level", split_axis=1, concat_axis=0, tiled=True)
    pos = tokens // n
    spot = jnp.arange(frames, dtype=jnp.int32)
    for step in range(STEPS):
        hin = current.astype(jnp.float32) + cond[:, None, :]
        power = jnp.mean(hin * hin, axis=-1, keepdims=True)
        normed = (hin * lax.rsqrt(power + 1e-06) * norm_gain).astype(jnp.bfloat16)
        flat = normed.reshape(-1, width)

        def project(weight):
            out = jnp.dot(flat, weight, preferred_element_type=jnp.float32)
            return out.astype(jnp.bfloat16).reshape(frames, pos, heads, DH).astype(jnp.float32)

        edge = ((BAND, BAND), (0, 0), (0, 0), (0, 0))
        query = project(w_query)
        keys = jnp.pad(project(w_key), edge)
        values = jnp.pad(project(w_value), edge)
        scores = []
        masks = []
        for offset in range(-BAND, BAND + 1):
            raw = jnp.sum(query * keys[BAND + offset : BAND + offset + frames], -1) / DH**0.5
            valid = (offset >= -reach) & (spot + offset >= 0) & (spot + offset < frames)
            scores.append(jnp.where(valid[:, None, None], raw, -1e30))
            masks.append(valid.astype(jnp.float32)[:, None, None])
        scores = jnp.stack(scores)
        expo = jnp.exp(scores - jnp.max(scores, axis=0)[None]) * jnp.stack(masks)
        weights = (expo / jnp.sum(expo, axis=0)[None]).astype(jnp.bfloat16).astype(jnp.float32)
        attended = jnp.zeros((frames, pos, heads, DH), jnp.float32)
        for slot in range(SPAN):
            attended = attended + weights[slot][..., None] * values[slot : slot + frames]
        noise = jnp.dot(
            attended.astype(jnp.bfloat16).reshape(-1, width),
            w_out,
            preferred_element_type=jnp.float32,
        ).reshape(frames, pos, width)
        updated = current.astype(jnp.float32) - rate[:, None, None] * noise
        current = jnp.roll(updated.astype(jnp.bfloat16), fdev, axis=0)
    return lax.all_to_all(current, "level", split_axis=0, concat_axis=1, tiled=True)


def per_device(latents, *rest):
    n = lax.axis_size("level")
    tokens = latents.shape[1]
    fits = tokens % (8 * HALVES * n) == 0 and latents.shape[0] * n % 8 == 0
    if fits and n & (n - 1) == 0:
        return fused(latents, *rest)
    return general(latents, *rest)


def solution(mesh):
    in_specs = (
        P(("groups", "level"), None, None),
        P(("groups", "level")),
        P(("groups", "level")),
        P("groups"),
        P("level", None),
        P(),
        P(),
        P(),
        P(),
        P(),
        P(),
        P(),
        P(),
    )
    out_specs = P(("groups", "level"), None, None)
    return jax.shard_map(
        per_device, mesh=mesh, in_specs=in_specs, out_specs=out_specs, check_vma=False
    )
```

```python
import functools

import jax
import jax.numpy as jnp
from jax import lax
from jax.experimental import pallas as pl
from jax.experimental.pallas import tpu as pltpu
from jax.sharding import PartitionSpec as P

DH = 64
BAND = 2
STEPS = 3
SPAN = 2 * BAND + 1
MESH = pl.DeviceIdType.MESH


def queue_kernel(
    n,
    x_hbm,
    level_hbm,
    reach_hbm,
    ids_hbm,
    table_hbm,
    proj_hbm,
    embed_hbm,
    srate_hbm,
    gain_hbm,
    wq_hbm,
    wk_hbm,
    wv_hbm,
    wo_hbm,
    out_hbm,
    recv,
    xa,
    xb,
    xo,
    q_s,
    k_s,
    v_s,
    part,
    att,
    table,
    proj,
    embed,
    gain_s,
    plain,
    wo,
    spread,
    wop,
    level_s,
    reach_s,
    ids_s,
    srate_s,
    pool,
    metas,
    metas_s,
    cond,
    rate,
    mask,
    perm,
    unperm,
    gather,
    x_send,
    x_recv,
    p_send,
    p_recv,
    m_send,
    m_recv,
    o_send,
    o_recv,
    local,
):
    me = lax.axis_index("level")
    fdev = x_hbm.shape[0]
    halves, frames, pos, width = recv.shape
    rows = frames * pos
    pad = BAND * pos
    barrier = pltpu.get_barrier_semaphore()
    for hop in range(1, n):
        pl.semaphore_signal(
            barrier, inc=1, device_id={"level": lax.rem(me + hop, n)}, device_id_type=MESH
        )
    mine = pl.ds(me * fdev, fdev)
    pairs = [
        (level_hbm, level_s),
        (reach_hbm, reach_s),
        (ids_hbm, ids_s),
        (srate_hbm, srate_s),
        (table_hbm, table),
        (embed_hbm, embed),
        (gain_hbm, gain_s),
        (proj_hbm, proj),
        (wq_hbm, plain.at[0]),
        (wk_hbm, plain.at[1]),
        (wv_hbm, plain.at[2]),
        (wo_hbm, wo),
    ] + [(x_hbm.at[:, me, h], recv.at[h, mine]) for h in range(halves)]
    stage = [
        pltpu.make_async_copy(src, dst, local.at[slot]) for slot, (src, dst) in enumerate(pairs)
    ]
    for copy in stage:
        copy.start()

    def x_copy(h, peer, owner):
        return pltpu.make_async_remote_copy(
            src_ref=x_hbm.at[:, peer, h],
            dst_ref=recv.at[h, pl.ds(owner * fdev, fdev)],
            send_sem=x_send.at[h, peer],
            recv_sem=x_recv.at[h, owner],
            device_id={"level": peer},
            device_id_type=MESH,
        )

    def p_copy(peer, owner):
        return pltpu.make_async_remote_copy(
            src_ref=pool.at[owner],
            dst_ref=pool.at[owner],
            send_sem=p_send.at[peer],
            recv_sem=p_recv.at[owner],
            device_id={"level": peer},
            device_id_type=MESH,
        )

    def m_copy(peer, owner):
        return pltpu.make_async_remote_copy(
            src_ref=metas.at[owner],
            dst_ref=metas.at[owner],
            send_sem=m_send.at[peer],
            recv_sem=m_recv.at[owner],
            device_id={"level": peer},
            device_id_type=MESH,
        )

    def o_copy(h, section, owner, peer):
        return pltpu.make_async_remote_copy(
            src_ref=xo.at[h, pl.ds(section * fdev, fdev)],
            dst_ref=out_hbm.at[:, owner, h],
            send_sem=o_send.at[h, peer],
            recv_sem=o_recv.at[h, owner],
            device_id={"level": peer},
            device_id_type=MESH,
        )

    def flip(bits):
        other = me
        for place in range(n.bit_length()):
            if bits >> place & 1:
                bit = lax.rem(lax.div(me, 1 << place), 2)
                other = other + (1 - 2 * bit) * (1 << place)
        return other

    order = sorted(range(1, n), key=lambda bits: (bits < 4, not bits & 2, bits))
    peers = [flip(bits) for bits in order]
    pl.semaphore_wait(barrier, n - 1)
    early = 4
    for peer in peers[:early]:
        x_copy(0, peer, me).start()

    stage[0].wait()
    stage[1].wait()
    lane = lax.broadcasted_iota(jnp.int32, (1, 128), 1)
    fact = jnp.zeros((1, 128), jnp.int32)
    for f in range(fdev):
        fact = jnp.where(lane == f, level_s[f], fact)
        fact = jnp.where(lane == fdev + f, reach_s[f], fact)
    metas[me] = fact
    for peer in peers:
        m_copy(peer, me).start()

    vocab = table.shape[0]
    stage[2].wait()
    first_id = me * vocab
    text_tokens = ids_s.shape[0]
    sublane = lax.broadcasted_iota(jnp.int32, (8, 1), 0)
    spots = lax.broadcasted_iota(jnp.int32, (8, vocab), 1)
    counts = jnp.zeros((8, vocab), jnp.float32)
    for first_token in range(0, text_tokens, 8):
        wanted = jnp.full((8, 1), -1, jnp.int32)
        for token in range(first_token, min(first_token + 8, text_tokens)):
            wanted = jnp.where(sublane == token - first_token, ids_s[token] - first_id, wanted)
        counts = counts + jnp.where(spots == wanted, 1.0, 0.0)
    counts = jnp.concatenate([counts, jnp.zeros((8, vocab), jnp.float32)], axis=0).astype(
        jnp.bfloat16
    )
    stage[4].wait()
    partial = jnp.dot(counts, table[...], preferred_element_type=jnp.float32)
    pool[me] = jnp.sum(partial[0:8], axis=0, keepdims=True)
    for peer in peers:
        p_copy(peer, me).start()
    for peer in peers[early:]:
        x_copy(0, peer, me).start()

    heads = width // DH
    per = 128 // heads
    wide = k_s.shape[1]
    blocks_w = wide // 128

    def source(place):
        block = lax.shift_right_logical(place, 7)
        spot = place - block * 128
        head = jnp.zeros(place.shape, jnp.int32)
        for number in range(1, heads + 1):
            head = head + jnp.where(spot >= number * per, 1, 0)
        dim = block * per + spot - head * per
        return jnp.where((head < heads) & (dim < DH), head * DH + dim, -1)

    strip = 64

    def build_perm(index, carry):
        at = pl.multiple_of(index * strip, strip)
        row = lax.broadcasted_iota(jnp.int32, (strip, wide), 0) + at
        here = row == source(lax.broadcasted_iota(jnp.int32, (1, wide), 1))
        perm[pl.ds(at, strip)] = jnp.where(here, 1.0, 0.0).astype(jnp.bfloat16)
        return carry

    def build_unperm(index, carry):
        at = pl.multiple_of(index * strip, strip)
        col = lax.broadcasted_iota(jnp.int32, (strip, width), 1)
        here = col == source(lax.broadcasted_iota(jnp.int32, (strip, 1), 0) + at)
        unperm[pl.ds(at, strip)] = jnp.where(here, 1.0, 0.0).astype(jnp.bfloat16)
        return carry

    lax.fori_loop(0, width // strip, build_perm, 0)
    lax.fori_loop(0, wide // strip, build_unperm, 0)

    def head_of(shape, axis):
        place = lax.broadcasted_iota(jnp.int32, shape, axis)
        head = jnp.where(place >= 128, heads + 1, 0)
        for number in range(1, heads + 1):
            head = head + jnp.where((place & 127) >= number * per, 1, 0)
        return jnp.where((place & 127) >= heads * per, -1 - axis, head)

    gather[...] = jnp.where(head_of((256, 1), 0) == head_of((1, 256), 1), 1.0 / DH**0.5, 0.0).astype(
        jnp.bfloat16
    )
    edge = jnp.zeros((pad, wide), jnp.float32)
    for buffer in (k_s, v_s):
        buffer[0:pad] = edge
        buffer[rows + pad : rows + 2 * pad] = edge
    for slot in (8, 9, 10, 11):
        stage[slot].wait()

    def respread(index, carry):
        spread[index] = jnp.dot(
            plain[index], perm[...], preferred_element_type=jnp.float32
        ).astype(jnp.bfloat16)
        return carry

    lax.fori_loop(0, 3, respread, 0)
    for h in range(1, halves):
        for peer in peers:
            x_copy(h, peer, me).start()
    wop[...] = jnp.dot(unperm[...], wo[...], preferred_element_type=jnp.float32).astype(
        jnp.bfloat16
    )

    for peer in peers:
        m_copy(peer, peer).wait_recv()
    told = pltpu.make_async_copy(metas, metas_s, local.at[12 + 2 * halves])
    told.start()
    for slot in (3, 5, 6, 7):
        stage[slot].wait()
    told.wait()
    for frame in range(frames):
        s, f = divmod(frame, fdev)
        level = metas_s[s, 0, f]
        reach = metas_s[s, 0, fdev + f]
        rate[frame] = jnp.full((1, width), srate_s[level], jnp.float32)
        cond[frame] = embed[pl.ds(level, 1), :]
        for slot in range(SPAN):
            offset = slot - BAND
            inside = 0 <= frame + offset < frames
            if offset < 0 and inside:
                value = jnp.where(reach >= -offset, 0.0, -1e30)
            else:
                value = 0.0 if inside else -1e30
            mask[slot, frame] = jnp.full((1, 128), value, jnp.float32)

    for peer in peers:
        p_copy(peer, peer).wait_recv()
    pooled = jnp.sum(pool[...], axis=0) / float(text_tokens)
    pooled = jnp.broadcast_to(pooled, (16, pooled.shape[1])).astype(jnp.bfloat16)
    text = jnp.dot(pooled, proj[...], preferred_element_type=jnp.float32)[0:1]
    cond[...] = cond[...] + text.reshape(1, 1, width)

    gain = gain_s[...].reshape(1, 1, width)
    cell = 8

    def project(current):
        hin = current + cond[...]
        power = jnp.mean(hin * hin, axis=-1, keepdims=True)
        flat = (hin * lax.rsqrt(power + 1e-06) * gain).reshape(rows, width).astype(jnp.bfloat16)
        q_s[...] = jnp.dot(flat, spread[0], preferred_element_type=jnp.float32)
        k_s[pad : pad + rows] = jnp.dot(flat, spread[1], preferred_element_type=jnp.float32)
        v_s[pad : pad + rows] = jnp.dot(flat, spread[2], preferred_element_type=jnp.float32)

    def attend(current):
        size = cell * pos
        for first in range(0, frames, cell):
            start = first * pos
            for slot in range(SPAN):
                at = start + slot * pos
                total = None
                for block in range(blocks_w):
                    lanes = slice(block * 128, block * 128 + 128)
                    term = q_s[start : start + size, lanes] * k_s[at : at + size, lanes]
                    total = term if total is None else total + term
                part[start : start + size, slot * 128 : slot * 128 + 128] = total.astype(
                    jnp.bfloat16
                )
        raws = []
        for slot in range(0, SPAN, 2):
            lanes = min(2, SPAN - slot) * 128
            made = jnp.dot(
                part[:, slot * 128 : slot * 128 + lanes],
                gather[0:lanes, 0:lanes],
                preferred_element_type=jnp.float32,
            )
            raws.extend(made[:, at : at + 128] for at in range(0, lanes, 128))
        for first in range(0, frames, cell):
            start = first * pos
            scores = []
            for slot in range(SPAN):
                raw = raws[slot][start : start + size].reshape(cell, pos, 128)
                scores.append(raw + mask[slot, first : first + cell])
            top = functools.reduce(jnp.maximum, scores)
            expo = [jnp.exp(score - top) for score in scores]
            inverse = 1.0 / functools.reduce(jnp.add, expo)
            weights = [
                (one * inverse).reshape(size, 128).astype(jnp.bfloat16).astype(jnp.float32)
                for one in expo
            ]
            for block in range(blocks_w):
                lanes = slice(block * 128, block * 128 + 128)
                total = None
                for slot in range(SPAN):
                    at = start + slot * pos
                    term = weights[slot] * v_s[at : at + size, lanes]
                    total = term if total is None else total + term
                att[start : start + size, lanes] = total.astype(jnp.bfloat16)
        noise = jnp.dot(att[...], wop[...], preferred_element_type=jnp.float32)
        return current - rate[...] * noise.reshape(frames, pos, width)

    def half(h, carry):
        stage_x = pltpu.make_async_copy(x_hbm.at[:, me, h], recv.at[h, mine], local.at[12 + h])
        stage_x.wait()
        for peer in peers:
            x_copy(h, peer, peer).wait_recv()
        turn = fdev * pos
        for step in range(STEPS):
            last = step == STEPS - 1
            held = xa if step % 2 == 1 else xb
            fresh = xb if step % 2 == 1 else xa

            def load(first, count, step=step, held=held):
                if step == 0:
                    return recv[h, pl.ds(first, count)].astype(jnp.float32)
                start = pl.multiple_of(first * pos, 16)
                return (
                    held[pl.ds(start, count * pos)].astype(jnp.float32).reshape(count, pos, width)
                )

            project(load(0, frames))

            made = attend(load(0, frames))
            if last:
                xo[h] = made.astype(jnp.bfloat16)
            else:
                fresh[turn : turn + rows] = made.reshape(rows, width).astype(jnp.bfloat16)
            if not last:
                fresh[0:turn] = fresh[rows : rows + turn]
        for peer in peers:
            o_copy(h, lax.rem(peer + n - 1, n), me, peer).start()
        pltpu.make_async_copy(
            xo.at[h, pl.ds(lax.rem(me + n - 1, n) * fdev, fdev)],
            out_hbm.at[:, me, h],
            local.at[12 + halves + h],
        ).start()
        return carry

    lax.fori_loop(0, halves, half, 0)

    for h in range(halves):
        for peer in peers:
            x_copy(h, peer, me).wait_send()
    for peer in peers:
        m_copy(peer, me).wait_send()
        p_copy(peer, me).wait_send()
    for h in range(halves):
        pltpu.make_async_copy(
            xo.at[h, pl.ds(lax.rem(me + n - 1, n) * fdev, fdev)],
            out_hbm.at[:, me, h],
            local.at[12 + halves + h],
        ).wait()
        for peer in peers:
            o_copy(h, lax.rem(peer + n - 1, n), me, peer).wait_send()
            o_copy(h, lax.rem(me + n - 1, n), peer, me).wait_recv()


HALVES = 2
GRANT = 40 << 20


def fused(
    latents,
    levels,
    back_reach,
    text_ids,
    text_table,
    text_proj,
    level_embed,
    step_rate,
    norm_gain,
    w_query,
    w_key,
    w_value,
    w_out,
):
    n = lax.axis_size("level")
    fdev, tokens, width = latents.shape
    pos = tokens // (n * HALVES)
    frames = fdev * n
    rows = frames * pos
    bf16, f32, i32 = jnp.bfloat16, jnp.float32, jnp.int32
    anywhere = pl.BlockSpec(memory_space=pl.ANY)
    stored = pl.BlockSpec(memory_space=pltpu.HBM)
    dma = pltpu.SemaphoreType.DMA
    block = pltpu.VMEM((HALVES, frames, pos, width), bf16)
    rolled = pltpu.VMEM((rows + fdev * pos, width), bf16)
    wide = -(-DH // (128 // (width // DH))) * 128
    padded = pltpu.VMEM((rows + 2 * BAND * pos, wide), f32)
    square = pltpu.VMEM((width, width), bf16)
    out = pl.pallas_call(
        functools.partial(queue_kernel, n),
        out_shape=jax.ShapeDtypeStruct((fdev, n, HALVES, pos, width), bf16),
        in_specs=[stored] * 13,
        out_specs=anywhere,
        scratch_shapes=[
            block,
            rolled,
            rolled,
            block,
            pltpu.VMEM((rows, wide), f32),
            padded,
            padded,
            pltpu.VMEM((rows, SPAN * 128), bf16),
            pltpu.VMEM((rows, wide), bf16),
            pltpu.VMEM(text_table.shape, bf16),
            pltpu.VMEM(text_proj.shape, bf16),
            pltpu.VMEM(level_embed.shape, f32),
            pltpu.VMEM(norm_gain.shape, f32),
            pltpu.VMEM((3, width, width), bf16),
            square,
            pltpu.VMEM((3, width, wide), bf16),
            pltpu.VMEM((wide, width), bf16),
            pltpu.SMEM(levels.shape, i32),
            pltpu.SMEM(back_reach.shape, i32),
            pltpu.SMEM(text_ids.shape, i32),
            pltpu.SMEM(step_rate.shape, f32),
            pltpu.VMEM((n, 1, text_table.shape[1]), f32),
            pltpu.VMEM((n, 1, 128), i32),
            pltpu.SMEM((n, 1, 128), i32),
            pltpu.VMEM((frames, 1, width), f32),
            pltpu.VMEM((frames, 1, width), f32),
            pltpu.VMEM((SPAN, frames, 1, 128), f32),
            pltpu.VMEM((width, wide), bf16),
            pltpu.VMEM((wide, width), bf16),
            pltpu.VMEM((256, 256), bf16),
            dma((HALVES, n)),
            dma((HALVES, n)),
            dma((n,)),
            dma((n,)),
            dma((n,)),
            dma((n,)),
            dma((HALVES, n)),
            dma((HALVES, n)),
            dma((13 + 2 * HALVES,)),
        ],
        compiler_params=pltpu.CompilerParams(
            collective_id=0, has_side_effects=True, vmem_limit_bytes=GRANT
        ),
        name="queue",
    )(
        *(
            pltpu.with_memory_space_constraint(value, pltpu.HBM)
            for value in (
                latents.reshape(fdev, n, HALVES, pos, width),
                levels,
                back_reach,
                text_ids,
                text_table,
                text_proj,
                level_embed,
                step_rate,
                norm_gain,
                w_query,
                w_key,
                w_value,
                w_out,
            )
        )
    )
    return out.reshape(fdev, tokens, width)


def general(
    latents,
    levels,
    back_reach,
    text_ids,
    text_table,
    text_proj,
    level_embed,
    step_rate,
    norm_gain,
    w_query,
    w_key,
    w_value,
    w_out,
):
    n = lax.axis_size("level")
    index = lax.axis_index("level")
    fdev, tokens, width = latents.shape
    heads = width // DH
    frames = fdev * n
    vocab = text_table.shape[0]
    spots = index * vocab + jnp.arange(vocab, dtype=jnp.int32)
    counts = jnp.sum((text_ids[:, None] == spots[None, :]).astype(jnp.float32), axis=0)
    partial = jnp.dot(
        counts.astype(jnp.bfloat16)[None, :], text_table, preferred_element_type=jnp.float32
    )
    pooled = lax.psum(partial, "level") / text_ids.shape[0]
    text_vec = jnp.dot(pooled.astype(jnp.bfloat16), text_proj, preferred_element_type=jnp.float32)
    levels = lax.all_gather(levels, "level", tiled=True)
    reach = lax.all_gather(back_reach, "level", tiled=True)
    cond = level_embed[levels] + text_vec
    rate = step_rate[levels]
    current = lax.all_to_all(latents, "level", split_axis=1, concat_axis=0, tiled=True)
    pos = tokens // n
    spot = jnp.arange(frames, dtype=jnp.int32)
    for step in range(STEPS):
        hin = current.astype(jnp.float32) + cond[:, None, :]
        power = jnp.mean(hin * hin, axis=-1, keepdims=True)
        normed = (hin * lax.rsqrt(power + 1e-06) * norm_gain).astype(jnp.bfloat16)
        flat = normed.reshape(-1, width)

        def project(weight):
            out = jnp.dot(flat, weight, preferred_element_type=jnp.float32)
            return out.astype(jnp.bfloat16).reshape(frames, pos, heads, DH).astype(jnp.float32)

        edge = ((BAND, BAND), (0, 0), (0, 0), (0, 0))
        query = project(w_query)
        keys = jnp.pad(project(w_key), edge)
        values = jnp.pad(project(w_value), edge)
        scores = []
        masks = []
        for offset in range(-BAND, BAND + 1):
            raw = jnp.sum(query * keys[BAND + offset : BAND + offset + frames], -1) / DH**0.5
            valid = (offset >= -reach) & (spot + offset >= 0) & (spot + offset < frames)
            scores.append(jnp.where(valid[:, None, None], raw, -1e30))
            masks.append(valid.astype(jnp.float32)[:, None, None])
        scores = jnp.stack(scores)
        expo = jnp.exp(scores - jnp.max(scores, axis=0)[None]) * jnp.stack(masks)
        weights = (expo / jnp.sum(expo, axis=0)[None]).astype(jnp.bfloat16).astype(jnp.float32)
        attended = jnp.zeros((frames, pos, heads, DH), jnp.float32)
        for slot in range(SPAN):
            attended = attended + weights[slot][..., None] * values[slot : slot + frames]
        noise = jnp.dot(
            attended.astype(jnp.bfloat16).reshape(-1, width),
            w_out,
            preferred_element_type=jnp.float32,
        ).reshape(frames, pos, width)
        updated = current.astype(jnp.float32) - rate[:, None, None] * noise
        current = jnp.roll(updated.astype(jnp.bfloat16), fdev, axis=0)
    return lax.all_to_all(current, "level", split_axis=0, concat_axis=1, tiled=True)


def per_device(latents, *rest):
    n = lax.axis_size("level")
    tokens = latents.shape[1]
    fits = tokens % (8 * HALVES * n) == 0 and latents.shape[0] * n % 8 == 0
    if fits and n & (n - 1) == 0:
        return fused(latents, *rest)
    return general(latents, *rest)


def solution(mesh):
    in_specs = (
        P(("groups", "level"), None, None),
        P(("groups", "level")),
        P(("groups", "level")),
        P("groups"),
        P("level", None),
        P(),
        P(),
        P(),
        P(),
        P(),
        P(),
        P(),
        P(),
    )
    out_specs = P(("groups", "level"), None, None)
    return jax.shard_map(
        per_device, mesh=mesh, in_specs=in_specs, out_specs=out_specs, check_vma=False
    )
```
